512 devices in a mesh: module: 8 (over x, y_lo), store: 64 (over y_hi, z, core).
Axes of the slice: x: 4, y: 4 (y_hi: 2, y_lo: 2; y = y_hi * 2 + y_lo), z: 16, core: 2. Of those that a mesh axis runs over, the one named last changes fastest.
Arguments:
- token_factors: float32 [8, 8192, 128], P('module', 'store'), may hold values from -4 to 4
- query_tokens: int32 [64, 8], P('store'), may hold values from 1 to 64, 128 in all within a row
- fisher_inverse: float32 [8, 4096, 4096], P('module', 'store'), may hold values from -0.09375 to 0.09375
- train_grads: bfloat16 [8, 24576, 4096], P('module', 'store'), may hold values from -0.09375 to 0.09375
Outputs:
- scores: float32 [24576, 512], P('store', 'module')
The draws below stay inside these ranges and needn't reach their ends.
Inputs may be any that keep to these rules, and one draw needn't show every extreme that they name: `query_tokens`: each row (the queries of one index of store) holds 8 counts of at least 1 that sum to 128; in every row the largest count is exactly 64.
All inputs are finite; a program needn't handle non-finite values.
Results may differ from the reference program's by a relative error of at most 0.0029.
Values may be sent and summed in bfloat16 or wider, within the bound.
No kernel may reach another device: no remote copies, remote signals or barrier semaphores. Data moves between devices by JAX's collectives and lax.ppermute only.
A program may use at most 64 MiB of HBM per device.

```python
import math
import jax
import jax.numpy as jnp
import numpy as np
from jax import lax

RANK = 64
GRAD = 4096
QRY_DEV = 8
TOK_DEV = 128
MOST_TOK = 64
MODULES = 8
QUERIES = 512
TRAIN = 24576
TOKENS = 8192
N_STORE = 64


def levels(key, dims, shards, smallest, largest):
    gain, own = 1.0, jax.random.fold_in(key, 6)
    for axis_at, parts in shards:
        steps = jnp.exp(jax.random.uniform(jax.random.fold_in(own, axis_at), (parts,), jnp.float32, smallest / len(shards), largest / len(shards)))
        gain = gain * jnp.repeat(steps, dims[axis_at] // parts).reshape([-1 if axis == axis_at else 1 for axis in range(len(dims))])
    return gain


def split_up(number_of, total, limit, lean):
    weights = [(1 << 20) // math.isqrt(standing ** lean) + 1 for standing in range(2, number_of + 1)]
    rest, given = total - limit - (number_of - 1), [1] * (number_of - 1)
    while rest > 0:
        free = [i for i in range(number_of - 1) if given[i] < limit]
        whole, budget = sum([weights[i] for i in free]), rest
        for i in free:
            more = min(limit - given[i], max(1, budget * weights[i] // whole), rest)
            given[i] = given[i] + more
            rest = rest - more
    return np.array([limit] + given)


def uneven(own_key, amount, total, bound, skew):
    if amount == 2:
        one = jax.random.randint(own_key, (), max(1, total - bound), min(bound, total - 1) + 1)
        return jnp.stack([one, total - one])
    sizes = jnp.asarray(split_up(amount, total, bound, skew), jnp.int32)
    twos = (amount - 1) // 2
    source_of, sink = sizes[1:1 + 2 * twos:2], sizes[2:2 + 2 * twos:2]
    margin = jnp.minimum(source_of - 1, bound - sink)
    moved = jax.random.randint(jax.random.fold_in(own_key, 1), (twos,), 0, 1 << 20) % (margin + 1)
    sizes = sizes.at[1:1 + 2 * twos:2].set(source_of - moved).at[2:2 + 2 * twos:2].set(sink + moved)
    return sizes[jax.random.permutation(jax.random.fold_in(own_key, 2), amount)]


def noise(rng, shape, spread, reach, split=(), kind=jnp.bfloat16):
    result = jax.random.normal(rng, shape, jnp.float32) * spread
    if len(split) > 0:
        result = levels(rng, shape, split, -0.22, 0.18) * result
    return jnp.clip(result, min=-reach, max=reach).astype(kind)


def setup_inputs(seed: int = 0) -> dict:
    arg_keys = jax.random.split(jax.random.key(seed), 5)
    token_factors = noise(arg_keys[0], (MODULES, TOKENS, 2 * RANK), 0.5, 4.0, ((0, 8), (1, 64)), jnp.float32)
    query_tokens = jax.vmap(lambda own: uneven(own, QRY_DEV, TOK_DEV, MOST_TOK, 1))(jax.random.split(arg_keys[1], N_STORE)).reshape((N_STORE, QRY_DEV)).astype(jnp.int32)
    fisher_inverse = noise(arg_keys[2], (MODULES, GRAD, GRAD), GRAD ** -0.5, 0.09375, ((0, 8), (1, 64)), jnp.float32)
    train_grads = noise(arg_keys[3], (MODULES, TRAIN, GRAD), GRAD ** -0.5, 0.09375, ((0, 8), (1, 64)))
    return {"token_factors": token_factors, "query_tokens": query_tokens, "fisher_inverse": fisher_inverse, "train_grads": train_grads}


def grads_of(factors, counts):
    ends = jnp.cumsum(counts).astype(jnp.int32)
    starts = ends - counts
    position = jnp.arange(factors.shape[0], dtype=jnp.int32)
    owner = ((position[:, None] >= starts[None, :]) & (position[:, None] < ends[None, :])).astype(jnp.float32)
    inputs = factors[:, :RANK]
    outgrad = factors[:, RANK:]
    weighted = (owner[:, :, None] * outgrad[:, None, :]).reshape(factors.shape[0], counts.shape[0] * RANK)
    grads = lax.dot_general(weighted, inputs, (((0,), (0,)), ((), ())), precision=lax.Precision.HIGHEST, preferred_element_type=jnp.float32)
    return grads.reshape(counts.shape[0], RANK * RANK)


def reference(token_factors, query_tokens, fisher_inverse, train_grads):
    total = jnp.zeros((TRAIN, QUERIES), jnp.float32)
    for module_index in range(MODULES):
        blocks = token_factors[module_index].reshape(N_STORE, TOK_DEV, 2 * RANK)
        query_grad = jax.vmap(grads_of)(blocks, query_tokens).reshape(QUERIES, GRAD)
        conditioned = lax.dot_general(query_grad, fisher_inverse[module_index], (((1,), (1,)), ((), ())), precision=lax.Precision.HIGHEST, preferred_element_type=jnp.float32).astype(jnp.bfloat16)
        total = total + lax.dot_general(train_grads[module_index], conditioned, (((1,), (1,)), ((), ())), preferred_element_type=jnp.float32)
    return total
```

```python
import functools

import jax
import jax.numpy as jnp
from jax import lax
from jax.experimental import pallas as pl
from jax.experimental.pallas import tpu as pltpu
from jax.sharding import Mesh, PartitionSpec as P

AXES = ("x", "yl", "yh", "z", "c")
F32, BF16, I32, I16 = jnp.float32, jnp.bfloat16, jnp.int32, jnp.int16
NT = (((1,), (1,)), ((), ()))
VMEM = pltpu.VMEM


def exponent(largest):
    return jnp.floor(jnp.log2(jnp.maximum(largest, 1e-30))) - 13.0


def coded(x, k):
    return jnp.round(x * jnp.exp2(-k)).astype(I32).astype(I16)


def split(x):
    hi = x.astype(BF16)
    return hi, (x - hi.astype(F32)).astype(BF16)


def encode_kernel(counts_ref, tok_ref, out_ref, buf):
    buf[...] = tok_ref[...].T
    rank = buf.shape[0] // 2
    ins = buf[:rank, :]
    ogs = buf[rank:, :]
    k_in = exponent(jnp.max(jnp.abs(ins), axis=0, keepdims=True))
    k_og = exponent(jnp.max(jnp.abs(ogs), axis=0, keepdims=True))
    t = lax.broadcasted_iota(I32, (1, buf.shape[1]), 1)
    owner = jnp.zeros_like(t)
    end = 0
    for j in range(7):
        end = end + counts_ref[0, j]
        owner = owner + (t >= end).astype(I32)
    even = buf[pl.ds(rank, rank // 2, stride=2), :]
    odd = buf[pl.ds(rank + 1, rank // 2, stride=2), :]
    row = lax.broadcasted_iota(I32, (8, buf.shape[1]), 0)
    extra = jnp.where(row == 0, k_in, jnp.where(row == 1, k_og, owner.astype(F32)))
    out_ref[:rank, :] = coded(ins, k_in)
    out_ref[rank : rank + rank // 2, :] = coded(even, k_og)
    out_ref[rank + rank // 2 : 2 * rank, :] = coded(odd, k_og)
    out_ref[2 * rank :, :] = extra.astype(I32).astype(I16)


def condition_kernel(tok_ref, mine_ref, other_ref, out_ref, g_hi, g_lo, f_hi, f_lo):
    nz = tok_ref.shape[0]
    core = lax.axis_index("c")
    for ref, at in ((mine_ref, core), (other_ref, 1 - core)):
        rows = ref.shape[0]
        hi, lo = split(ref[...])
        at = pl.multiple_of(at * rows, rows)
        f_hi[pl.ds(at, rows), :] = hi
        f_lo[pl.ds(at, rows), :] = lo

    def block(z, yh):
        x = tok_ref[z, yh].astype(I32).astype(F32)
        s_in = jnp.exp2(x[128:129, :])
        s_og = jnp.exp2(x[129:130, :])
        owner = x[130:131, :]
        j = lax.broadcasted_iota(I32, (8, 128), 0).astype(F32)
        mask = jnp.where(owner == j, 1.0, 0.0)
        in_hi, in_lo = split(x[0:64, :] * s_in)
        zero = jnp.zeros((64, 128), BF16)

        def diagonal(v):
            return jnp.concatenate(
                [jnp.concatenate([v, zero], axis=1), jnp.concatenate([zero, v], axis=1)], axis=0
            )

        r_hi, r_lo = diagonal(in_hi), diagonal(in_lo)

        def spread(v):
            w = v * s_og
            hi = w.astype(BF16).astype(F32)
            lo = w - hi
            return [
                (u[:, None, :] * mask[None]).reshape(256, 128).astype(BF16) for u in (hi, lo)
            ]

        e_hi, e_lo = spread(x[64:96, :])
        o_hi, o_lo = spread(x[96:128, :])
        l_hi = jnp.concatenate([e_hi, o_hi], axis=1)
        l_lo = jnp.concatenate([e_lo, o_lo], axis=1)
        two = lax.dot_general(
            l_hi, jnp.concatenate([r_hi, r_lo], axis=0), NT, preferred_element_type=F32
        )
        one = lax.dot_general(l_lo, r_hi, NT, preferred_element_type=F32)
        return (two[:, :128] + two[:, 128:] + one).reshape(32, 8, 128)

    def step(s, carry):
        yh = s // (nz // 2)
        z = (s % (nz // 2)) * 2
        g = jnp.concatenate([block(z, yh), block(z + 1, yh)], axis=1)
        hi, lo = split(g)
        at = pl.multiple_of(s * 16, 16)
        for a in range(32):
            g_hi[pl.ds(at, 16), a * 128 : (a + 1) * 128] = hi[a]
            g_lo[pl.ds(at, 16), a * 128 : (a + 1) * 128] = lo[a]
        return carry

    lax.fori_loop(0, nz, step, 0)
    dot = functools.partial(lax.dot_general, dimension_numbers=NT, preferred_element_type=F32)
    p = dot(g_hi[...], f_hi[...]) + dot(g_lo[...], f_hi[...]) + dot(g_hi[...], f_lo[...])
    k = exponent(jnp.max(jnp.abs(p), axis=0, keepdims=True))
    rows = p.shape[0]
    out_ref[:rows, :] = coded(p, k)
    out_ref[rows:, :] = jnp.broadcast_to(k, (8, 128)).astype(I32).astype(I16)


def score_kernel(p_ref, t_ref, swapped_ref, out_ref, p_all, t_own, sem):
    nz = p_ref.shape[0]
    half = t_own.shape[1]
    yh = lax.axis_index("yh")
    copy = pltpu.make_async_copy(
        t_ref.at[:, pl.ds(pl.multiple_of(yh * half, half), half)], t_own, sem
    )
    copy.start()
    for z in range(nz):
        parts = []
        for c in range(2):
            v = p_ref[z, c].astype(I32).astype(F32)
            parts.append((v[:256, :] * jnp.exp2(v[256:257, :])).reshape(32, 8, 128))
        p_all[:, z * 128 : (z + 1) * 128] = (
            jnp.concatenate(parts, axis=1).reshape(512, 128).astype(BF16)
        )
    copy.wait()
    for ref, at in ((t_own, yh), (swapped_ref, 1 - yh)):
        s = lax.dot_general(p_all[...], ref[...], NT, preferred_element_type=F32).astype(BF16)
        for m in range(8):
            out_ref[m, at] = s[m * 64 : (m + 1) * 64, :]


def swap(x, axis):
    return lax.ppermute(x, axis, [(0, 1), (1, 0)])


def body(token_factors, query_tokens, fisher_inverse, train_grads):
    fisher = fisher_inverse[0]
    stored = train_grads[0]
    examples, grad = stored.shape
    half = grad // 2
    vm = pl.BlockSpec(memory_space=VMEM)

    tokens = pl.pallas_call(
        encode_kernel,
        out_shape=jax.ShapeDtypeStruct((136, 128), I16),
        in_specs=[pl.BlockSpec(memory_space=pltpu.SMEM), vm],
        out_specs=vm,
        scratch_shapes=[VMEM((128, 128), F32)],
    )(query_tokens, token_factors[0])
    tokens = lax.all_gather(tokens, "yh")
    yh = lax.axis_index("yh")
    swapped = swap(lax.dynamic_slice_in_dim(stored, (1 - yh) * half, half, 1), "yh")
    fisher_other = swap(fisher, "c")
    tokens = lax.all_gather(tokens, "z")

    conditioned = pl.pallas_call(
        condition_kernel,
        out_shape=jax.ShapeDtypeStruct((264, 128), I16),
        in_specs=[vm, vm, vm],
        out_specs=vm,
        scratch_shapes=[VMEM((256, grad), BF16)] * 2 + [VMEM((128, grad), BF16)] * 2,
    )(tokens, fisher, fisher_other)
    conditioned = lax.all_gather(conditioned, ("z", "c")).reshape(16, 2, 264, 128)

    partial = pl.pallas_call(
        score_kernel,
        out_shape=jax.ShapeDtypeStruct((8, 2, 64, examples), BF16),
        in_specs=[vm, pl.BlockSpec(memory_space=pl.ANY), vm],
        out_specs=vm,
        scratch_shapes=[
            VMEM((512, half), BF16),
            VMEM((examples, half), BF16),
            pltpu.SemaphoreType.DMA,
        ],
    )(conditioned, stored, swapped)
    partial = lax.all_to_all(
        partial.reshape(16, 64, examples), ("x", "yl", "yh"), 0, 0, tiled=True
    )
    return jnp.sum(partial.astype(F32), axis=0).T


def solution(mesh):
    fine = Mesh(mesh.devices.reshape(4, 2, 2, 16, 2), AXES)
    module, store = ("x", "yl"), ("yh", "z", "c")
    return jax.shard_map(
        body,
        mesh=fine,
        in_specs=(
            P(module, store, None),
            P(store, None),
            P(module, store, None),
            P(module, store, None),
        ),
        out_specs=P(store, module),
        check_vma=False,
    )
```

```python
import functools

import jax
import jax.numpy as jnp
from jax import lax
from jax.experimental import pallas as pl
from jax.experimental.pallas import tpu as pltpu
from jax.sharding import Mesh, PartitionSpec as P

AXES = ("x", "yl", "yh", "z", "c")
F32, BF16, I32, I16 = jnp.float32, jnp.bfloat16, jnp.int32, jnp.int16
NT = (((1,), (1,)), ((), ()))
VMEM = pltpu.VMEM


def exponent(largest):
    return jnp.floor(jnp.log2(jnp.maximum(largest, 1e-30))) - 13.0


def coded(x, k):
    return jnp.round(x * jnp.exp2(-k)).astype(I32).astype(I16)


def split(x):
    hi = x.astype(BF16)
    return hi, (x - hi.astype(F32)).astype(BF16)


def encode_kernel(counts_ref, tok_ref, t_ref, out_ref, half_ref, buf, sem):
    half = half_ref.shape[1]
    at = pl.multiple_of((1 - lax.axis_index("yh")) * half, half)
    copy = pltpu.make_async_copy(t_ref.at[:, pl.ds(at, half)], half_ref, sem)
    copy.start()
    buf[...] = tok_ref[...].T
    rank = buf.shape[0] // 2
    ins = buf[:rank, :]
    ogs = buf[rank:, :]
    k_in = exponent(jnp.max(jnp.abs(ins), axis=0, keepdims=True))
    k_og = exponent(jnp.max(jnp.abs(ogs), axis=0, keepdims=True))
    t = lax.broadcasted_iota(I32, (1, buf.shape[1]), 1)
    owner = jnp.zeros_like(t)
    end = 0
    for j in range(7):
        end = end + counts_ref[0, j]
        owner = owner + (t >= end).astype(I32)
    even = buf[pl.ds(rank, rank // 2, stride=2), :]
    odd = buf[pl.ds(rank + 1, rank // 2, stride=2), :]
    row = lax.broadcasted_iota(I32, (8, buf.shape[1]), 0)
    extra = jnp.where(row == 0, k_in, jnp.where(row == 1, k_og, owner.astype(F32)))
    out_ref[:rank, :] = coded(ins, k_in)
    out_ref[rank : rank + rank // 2, :] = coded(even, k_og)
    out_ref[rank + rank // 2 : 2 * rank, :] = coded(odd, k_og)
    out_ref[2 * rank :, :] = extra.astype(I32).astype(I16)
    copy.wait()


def condition_kernel(tok_ref, mine_ref, other_ref, out_ref, g_hi, g_lo, f_hi, f_lo):
    nz = tok_ref.shape[0]
    core = lax.axis_index("c")
    for ref, at in ((mine_ref, core), (other_ref, 1 - core)):
        rows = ref.shape[0]
        hi, lo = split(ref[...])
        at = pl.multiple_of(at * rows, rows)
        f_hi[pl.ds(at, rows), :] = hi
        f_lo[pl.ds(at, rows), :] = lo

    def block(z, yh):
        x = tok_ref[z, yh].astype(I32).astype(F32)
        s_in = jnp.exp2(x[128:129, :])
        s_og = jnp.exp2(x[129:130, :])
        owner = x[130:131, :]
        j = lax.broadcasted_iota(I32, (8, 128), 0).astype(F32)
        mask = jnp.where(owner == j, 1.0, 0.0)
        in_hi, in_lo = split(x[0:64, :] * s_in)
        zero = jnp.zeros((64, 128), BF16)

        def diagonal(v):
            return jnp.concatenate(
                [jnp.concatenate([v, zero], axis=1), jnp.concatenate([zero, v], axis=1)], axis=0
            )

        r_hi, r_lo = diagonal(in_hi), diagonal(in_lo)

        def spread(v):
            w = v * s_og
            hi = w.astype(BF16).astype(F32)
            lo = w - hi
            return [
                (u[:, None, :] * mask[None]).reshape(256, 128).astype(BF16) for u in (hi, lo)
            ]

        e_hi, e_lo = spread(x[64:96, :])
        o_hi, o_lo = spread(x[96:128, :])
        l_hi = jnp.concatenate([e_hi, o_hi], axis=1)
        l_lo = jnp.concatenate([e_lo, o_lo], axis=1)
        two = lax.dot_general(
            l_hi, jnp.concatenate([r_hi, r_lo], axis=0), NT, preferred_element_type=F32
        )
        one = lax.dot_general(l_lo, r_hi, NT, preferred_element_type=F32)
        return (two[:, :128] + two[:, 128:] + one).reshape(32, 8, 128)

    def step(s, carry):
        yh = s // (nz // 2)
        z = (s % (nz // 2)) * 2
        g = jnp.concatenate([block(z, yh), block(z + 1, yh)], axis=1)
        hi, lo = split(g)
        at = pl.multiple_of(s * 16, 16)
        for a in range(32):
            g_hi[pl.ds(at, 16), a * 128 : (a + 1) * 128] = hi[a]
            g_lo[pl.ds(at, 16), a * 128 : (a + 1) * 128] = lo[a]
        return carry

    lax.fori_loop(0, nz, step, 0)
    dot = functools.partial(lax.dot_general, dimension_numbers=NT, preferred_element_type=F32)
    p = dot(g_hi[...], f_hi[...]) + dot(g_lo[...], f_hi[...]) + dot(g_hi[...], f_lo[...])
    k = exponent(jnp.max(jnp.abs(p), axis=0, keepdims=True))
    rows = p.shape[0]
    out_ref[:rows, :] = coded(p, k)
    out_ref[rows:, :] = jnp.broadcast_to(k, (8, 128)).astype(I32).astype(I16)


def score_kernel(p_ref, t_ref, swapped_ref, out_ref, p_all):
    nz = p_ref.shape[0]
    half = swapped_ref.shape[1]
    yh = lax.axis_index("yh")
    for z in range(nz):
        parts = []
        for c in range(2):
            v = p_ref[z, c].astype(I32).astype(F32)
            parts.append((v[:256, :] * jnp.exp2(v[256:257, :])).reshape(32, 8, 128))
        p_all[:, z * 128 : (z + 1) * 128] = (
            jnp.concatenate(parts, axis=1).reshape(512, 128).astype(BF16)
        )
    own = t_ref[:, pl.ds(pl.multiple_of(yh * half, half), half)]
    for t, at in ((own, yh), (swapped_ref[...], 1 - yh)):
        s = lax.dot_general(p_all[...], t, NT, preferred_element_type=F32).astype(BF16)
        for m in range(8):
            out_ref[m, at] = s[m * 64 : (m + 1) * 64, :]


def grant(mib):
    return pltpu.CompilerParams(vmem_limit_bytes=mib << 20)


def swap(x, axis):
    return lax.ppermute(x, axis, [(0, 1), (1, 0)])


def body(token_factors, query_tokens, fisher_inverse, train_grads):
    fisher = fisher_inverse[0]
    stored = train_grads[0]
    examples, grad = stored.shape
    half = grad // 2
    vm = pl.BlockSpec(memory_space=VMEM)

    tokens, swapped = pl.pallas_call(
        encode_kernel,
        out_shape=(
            jax.ShapeDtypeStruct((136, 128), I16),
            jax.ShapeDtypeStruct((examples, half), BF16),
        ),
        in_specs=[
            pl.BlockSpec(memory_space=pltpu.SMEM),
            vm,
            pl.BlockSpec(memory_space=pl.ANY),
        ],
        out_specs=(vm, vm),
        scratch_shapes=[VMEM((128, 128), F32), pltpu.SemaphoreType.DMA],
        compiler_params=grant(60),
    )(query_tokens, token_factors[0], stored)
    tokens = lax.all_gather(tokens, "yh")
    tokens, swapped, fisher = lax.optimization_barrier((tokens, swapped, fisher))
    swapped = swap(swapped, "yh")
    fisher_other = swap(fisher, "c")
    tokens = lax.all_gather(tokens, "z")

    conditioned = pl.pallas_call(
        condition_kernel,
        out_shape=jax.ShapeDtypeStruct((264, 128), I16),
        in_specs=[vm, vm, vm],
        out_specs=vm,
        scratch_shapes=[VMEM((256, grad), BF16)] * 2 + [VMEM((128, grad), BF16)] * 2,
        compiler_params=grant(24),
    )(tokens, fisher, fisher_other)
    conditioned = lax.all_gather(conditioned, ("z", "c")).reshape(16, 2, 264, 128)

    partial = pl.pallas_call(
        score_kernel,
        out_shape=jax.ShapeDtypeStruct((8, 2, 64, examples), BF16),
        in_specs=[vm, vm, vm],
        out_specs=vm,
        scratch_shapes=[VMEM((512, half), BF16)],
        compiler_params=grant(24),
    )(conditioned, stored, swapped)
    partial = lax.all_to_all(
        partial.reshape(16, 64, examples), ("x", "yl", "yh"), 0, 0, tiled=True
    )
    return jnp.sum(partial.astype(F32), axis=0).T


def solution(mesh):
    fine = Mesh(mesh.devices.reshape(4, 2, 2, 16, 2), AXES)
    module, store = ("x", "yl"), ("yh", "z", "c")
    return jax.shard_map(
        body,
        mesh=fine,
        in_specs=(
            P(module, store, None),
            P(store, None),
            P(module, store, None),
            P(module, store, None),
        ),
        out_specs=P(store, module),
        check_vma=False,
    )
```

```python
import functools

import jax
import jax.numpy as jnp
from jax import lax
from jax.experimental import pallas as pl
from jax.experimental.pallas import tpu as pltpu
from jax.sharding import Mesh, PartitionSpec as P

AXES = ("x", "yl", "yh", "z", "c")
F32, BF16, I32, I16 = jnp.float32, jnp.bfloat16, jnp.int32, jnp.int16
NT = (((1,), (1,)), ((), ()))
VMEM = pltpu.VMEM
UNROLL = 8
CHUNKS = 6


def exponent(largest):
    return jnp.floor(jnp.log2(jnp.maximum(largest, 1e-30))) - 13.0


def coded(x, k):
    return jnp.round(x * jnp.exp2(-k)).astype(I32).astype(I16)


def split(x):
    hi = x.astype(BF16)
    return hi, (x - hi.astype(F32)).astype(BF16)


def encode_kernel(counts_ref, tok_ref, t_ref, out_ref, half_ref, buf, rows, load, store):
    half = half_ref.shape[1]
    at = pl.multiple_of((1 - lax.axis_index("yh")) * half, half)
    chunk = rows.shape[0] // CHUNKS
    pieces = [pl.ds(i * chunk, chunk) for i in range(CHUNKS)]
    loads = [
        pltpu.make_async_copy(t_ref.at[piece, pl.ds(at, half)], rows.at[piece], load.at[i])
        for i, piece in enumerate(pieces)
    ]
    stores = [
        pltpu.make_async_copy(rows.at[piece], half_ref.at[piece], store.at[i])
        for i, piece in enumerate(pieces)
    ]
    for copy in loads:
        copy.start()
    buf[...] = tok_ref[...].T
    rank = buf.shape[0] // 2
    ins = buf[:rank, :]
    ogs = buf[rank:, :]
    k_in = exponent(jnp.max(jnp.abs(ins), axis=0, keepdims=True))
    k_og = exponent(jnp.max(jnp.abs(ogs), axis=0, keepdims=True))
    t = lax.broadcasted_iota(I32, (1, buf.shape[1]), 1)
    owner = jnp.zeros_like(t)
    for i in range(CHUNKS // 2):
        loads[i].wait()
        stores[i].start()
    end = 0
    for j in range(7):
        end = end + counts_ref[0, j]
        owner = owner + (t >= end).astype(I32)
    even = buf[pl.ds(rank, rank // 2, stride=2), :]
    odd = buf[pl.ds(rank + 1, rank // 2, stride=2), :]
    row = lax.broadcasted_iota(I32, (8, buf.shape[1]), 0)
    extra = jnp.where(row == 0, k_in, jnp.where(row == 1, k_og, owner.astype(F32)))
    out_ref[:rank, :] = coded(ins, k_in)
    out_ref[rank : rank + rank // 2, :] = coded(even, k_og)
    out_ref[rank + rank // 2 : 2 * rank, :] = coded(odd, k_og)
    out_ref[2 * rank :, :] = extra.astype(I32).astype(I16)
    for i in range(CHUNKS // 2, CHUNKS):
        loads[i].wait()
        stores[i].start()
    for copy in stores:
        copy.wait()


def condition_kernel(tok_ref, mine_ref, other_ref, out_ref, grads, wide):
    nz = tok_ref.shape[0]
    core = lax.axis_index("c")
    j = lax.broadcasted_iota(I32, (8, 128), 0).astype(F32)

    def block(z, yh, slot):
        x = tok_ref[z, core, yh].astype(I32).astype(F32)
        mask = jnp.where(x[130:131, :] == j, 1.0, 0.0)
        in_hi, in_lo = split(x[0:64, :] * jnp.exp2(x[128:129, :]))
        zero = jnp.zeros((64, 128), BF16)

        def diagonal(v):
            return jnp.concatenate(
                [jnp.concatenate([v, zero], axis=1), jnp.concatenate([zero, v], axis=1)], axis=0
            )

        r_hi, r_lo = diagonal(in_hi), diagonal(in_lo)
        w = x[64:128, :] * jnp.exp2(x[129:130, :])
        hi = w.astype(BF16).astype(F32)
        wide[slot, 0] = hi
        wide[slot, 1] = w - hi

        def spread(part):
            halves = []
            for odd in range(2):
                rows = [
                    wide[slot, part, pl.ds(odd * 32 + a, 8, stride=0), :] * mask
                    for a in range(32)
                ]
                halves.append(jnp.concatenate(rows, axis=0).astype(BF16))
            return jnp.concatenate(halves, axis=1)

        two = lax.dot_general(
            spread(0), jnp.concatenate([r_hi, r_lo], axis=0), NT, preferred_element_type=F32
        )
        one = lax.dot_general(spread(1), r_hi, NT, preferred_element_type=F32)
        g = two[:, :128] + two[:, 128:] + one
        at = pl.multiple_of((yh * nz + z) * 8, 8)
        for a in range(32):
            grads[pl.ds(at, 8), a * 128 : (a + 1) * 128] = g[a * 8 : (a + 1) * 8, :]

    def step(s, carry):
        for i in range(UNROLL):
            block(s * (UNROLL // 2) + i // 2, i % 2, i)
        return carry

    lax.fori_loop(0, 2 * nz // UNROLL, step, 0)
    dot = functools.partial(lax.dot_general, dimension_numbers=NT, preferred_element_type=F32)
    wide_rows, width = mine_ref.shape[0], 512
    p = jnp.zeros((grads.shape[0], 2 * wide_rows), F32)
    for at in range(0, grads.shape[1], width):
        columns = slice(at, at + width)
        g_hi, g_lo = split(grads[:, columns])
        f = jnp.concatenate([mine_ref[:, columns], other_ref[:, columns]], axis=0)
        f_hi, f_lo = split(f)
        two = dot(g_hi, jnp.concatenate([f_hi, f_lo], axis=0))
        one = dot(g_lo, f_hi)
        p = p + (two[:, : 2 * wide_rows] + two[:, 2 * wide_rows :] + one)
    p = jnp.where(core == 0, p, pltpu.roll(p, wide_rows, 1))
    k = exponent(jnp.max(jnp.abs(p), axis=0, keepdims=True))
    rows = p.shape[0]
    out_ref[:rows, :] = coded(p, k)
    out_ref[rows:, :] = jnp.broadcast_to(k, (8, 128)).astype(I32).astype(I16)


def score_kernel(p_ref, t_ref, swapped_ref, out_ref, p_all):
    nz = p_ref.shape[0]
    half = swapped_ref.shape[1]
    yh = lax.axis_index("yh")
    for z in range(nz):
        parts = []
        for c in range(2):
            v = p_ref[z, c].astype(I32).astype(F32)
            parts.append((v[:256, :] * jnp.exp2(v[256:257, :])).reshape(32, 8, 128))
        p_all[:, z * 128 : (z + 1) * 128] = (
            jnp.concatenate(parts, axis=1).reshape(512, 128).astype(BF16)
        )
    own = t_ref[:, pl.ds(pl.multiple_of(yh * half, half), half)]
    for t, at in ((own, yh), (swapped_ref[...], 1 - yh)):
        s = lax.dot_general(p_all[...], t, NT, preferred_element_type=F32).astype(BF16)
        for m in range(8):
            out_ref[m, at] = s[m * 64 : (m + 1) * 64, :]


def grant(mib):
    return pltpu.CompilerParams(vmem_limit_bytes=mib << 20)


def swap(x, axis):
    return lax.ppermute(x, axis, [(0, 1), (1, 0)])


def body(token_factors, query_tokens, fisher_inverse, train_grads):
    fisher = fisher_inverse[0]
    stored = train_grads[0]
    examples, grad = stored.shape
    half = grad // 2
    vm = pl.BlockSpec(memory_space=VMEM)

    tokens, swapped = pl.pallas_call(
        encode_kernel,
        out_shape=(
            jax.ShapeDtypeStruct((136, 128), I16),
            jax.ShapeDtypeStruct((examples, half), BF16),
        ),
        in_specs=[
            pl.BlockSpec(memory_space=pltpu.SMEM),
            vm,
            pl.BlockSpec(memory_space=pl.ANY),
        ],
        out_specs=(vm, pl.BlockSpec(memory_space=pl.ANY)),
        scratch_shapes=[
            VMEM((128, 128), F32),
            VMEM((examples, half), BF16),
            pltpu.SemaphoreType.DMA((CHUNKS,)),
            pltpu.SemaphoreType.DMA((CHUNKS,)),
        ],
        compiler_params=grant(60),
    )(query_tokens, token_factors[0], stored)
    tokens = lax.all_gather(tokens, "yh")
    tokens, swapped, fisher = lax.optimization_barrier((tokens, swapped, fisher))
    swapped = swap(swapped, "yh")
    fisher_other = swap(fisher, "c")
    tokens = lax.all_gather(tokens, ("z", "c")).reshape(16, 2, 2, 136, 128)

    conditioned = pl.pallas_call(
        condition_kernel,
        out_shape=jax.ShapeDtypeStruct((264, 128), I16),
        in_specs=[vm, vm, vm],
        out_specs=vm,
        scratch_shapes=[VMEM((256, grad), F32), VMEM((UNROLL, 2, 64, 128), F32)],
        compiler_params=grant(24),
    )(tokens, fisher, fisher_other)
    conditioned = lax.all_gather(conditioned, ("z", "c")).reshape(16, 2, 264, 128)

    partial = pl.pallas_call(
        score_kernel,
        out_shape=jax.ShapeDtypeStruct((8, 2, 64, examples), BF16),
        in_specs=[vm, vm, vm],
        out_specs=vm,
        scratch_shapes=[VMEM((512, half), BF16)],
        compiler_params=grant(24),
    )(conditioned, stored, swapped)
    partial = lax.all_to_all(
        partial.reshape(16, 64, examples), ("x", "yl", "yh"), 0, 0, tiled=True
    )
    return jnp.sum(partial.astype(F32), axis=0).T


def solution(mesh):
    fine = Mesh(mesh.devices.reshape(4, 2, 2, 16, 2), AXES)
    module, store = ("x", "yl"), ("yh", "z", "c")
    return jax.shard_map(
        body,
        mesh=fine,
        in_specs=(
            P(module, store, None),
            P(store, None),
            P(module, store, None),
            P(module, store, None),
        ),
        out_specs=P(store, module),
        check_vma=False,
    )
```

```python
import functools

import jax
import jax.numpy as jnp
from jax import lax
from jax.experimental import pallas as pl
from jax.experimental.pallas import tpu as pltpu
from jax.sharding import Mesh, PartitionSpec as P

AXES = ("x", "yl", "yh", "z", "c")
F32, BF16, I32, I16 = jnp.float32, jnp.bfloat16, jnp.int32, jnp.int16
NT = (((1,), (1,)), ((), ()))
VMEM = pltpu.VMEM
UNROLL = 8
ENCODE_MIB = 60


def exponent(largest):
    return jnp.floor(jnp.log2(jnp.maximum(largest, 1e-30))) - 13.0


def coded(x, k):
    return jnp.round(x * jnp.exp2(-k)).astype(I32).astype(I16)


def split(x):
    hi = x.astype(BF16)
    return hi, (x - hi.astype(F32)).astype(BF16)


def encode_kernel(counts_ref, tok_ref, out_ref, buf):
    buf[...] = tok_ref[...].T
    rank = buf.shape[0] // 2
    ins = buf[:rank, :]
    ogs = buf[rank:, :]
    k_in = exponent(jnp.max(jnp.abs(ins), axis=0, keepdims=True))
    k_og = exponent(jnp.max(jnp.abs(ogs), axis=0, keepdims=True))
    t = lax.broadcasted_iota(I32, (1, buf.shape[1]), 1)
    owner = jnp.zeros_like(t)
    end = 0
    for j in range(7):
        end = end + counts_ref[0, j]
        owner = owner + (t >= end).astype(I32)
    even = buf[pl.ds(rank, rank // 2, stride=2), :]
    odd = buf[pl.ds(rank + 1, rank // 2, stride=2), :]
    row = lax.broadcasted_iota(I32, (8, buf.shape[1]), 0)
    extra = jnp.where(row == 0, k_in, jnp.where(row == 1, k_og, owner.astype(F32)))
    out_ref[:rank, :] = coded(ins, k_in)
    out_ref[rank : rank + rank // 2, :] = coded(even, k_og)
    out_ref[rank + rank // 2 : 2 * rank, :] = coded(odd, k_og)
    out_ref[2 * rank :, :] = extra.astype(I32).astype(I16)


def half_kernel(t_ref, tokens_ref, half_ref):
    half = half_ref.shape[1]
    at = pl.multiple_of((1 - lax.axis_index("yh")) * half, half)
    half_ref[...] = t_ref[:, pl.ds(at, half)]


def condition_kernel(tok_ref, mine_ref, other_ref, out_ref, grads, wide):
    nz = tok_ref.shape[0]
    core, home = lax.axis_index("c"), lax.axis_index("yh")
    j = lax.broadcasted_iota(I32, (8, 128), 0).astype(F32)

    def block(z, away, slot):
        x = tok_ref[z, away].astype(I32).astype(F32)
        mask = jnp.where(x[130:131, :] == j, 1.0, 0.0)
        in_hi, in_lo = split(x[0:64, :] * jnp.exp2(x[128:129, :]))
        zero = jnp.zeros((64, 128), BF16)

        def diagonal(v):
            return jnp.concatenate(
                [jnp.concatenate([v, zero], axis=1), jnp.concatenate([zero, v], axis=1)], axis=0
            )

        r_hi, r_lo = diagonal(in_hi), diagonal(in_lo)
        w = x[64:128, :] * jnp.exp2(x[129:130, :])
        hi = w.astype(BF16).astype(F32)
        wide[slot, 0] = hi
        wide[slot, 1] = w - hi

        def spread(part):
            halves = []
            for odd in range(2):
                rows = [
                    wide[slot, part, pl.ds(odd * 32 + a, 8, stride=0), :] * mask
                    for a in range(32)
                ]
                halves.append(jnp.concatenate(rows, axis=0).astype(BF16))
            return jnp.concatenate(halves, axis=1)

        two = lax.dot_general(
            spread(0), jnp.concatenate([r_hi, r_lo], axis=0), NT, preferred_element_type=F32
        )
        one = lax.dot_general(spread(1), r_hi, NT, preferred_element_type=F32)
        g = two[:, :128] + two[:, 128:] + one
        yh = 1 - home if away else home
        at = pl.multiple_of((yh * nz + z) * 8, 8)
        for a in range(32):
            grads[pl.ds(at, 8), a * 128 : (a + 1) * 128] = g[a * 8 : (a + 1) * 8, :]

    def step(s, carry):
        for i in range(UNROLL):
            block(s * (UNROLL // 2) + i // 2, i % 2, i)
        return carry

    lax.fori_loop(0, 2 * nz // UNROLL, step, 0)
    dot = functools.partial(lax.dot_general, dimension_numbers=NT, preferred_element_type=F32)
    wide_rows, width = mine_ref.shape[0], 512
    p = jnp.zeros((grads.shape[0], 2 * wide_rows), F32)
    for at in range(0, grads.shape[1], width):
        columns = slice(at, at + width)
        g_hi, g_lo = split(grads[:, columns])
        f = jnp.concatenate([mine_ref[:, columns], other_ref[:, columns]], axis=0)
        f_hi, f_lo = split(f)
        two = dot(g_hi, jnp.concatenate([f_hi, f_lo], axis=0))
        one = dot(g_lo, f_hi)
        p = p + (two[:, : 2 * wide_rows] + two[:, 2 * wide_rows :] + one)
    p = jnp.where(core == 0, p, pltpu.roll(p, wide_rows, 1))
    k = exponent(jnp.max(jnp.abs(p), axis=0, keepdims=True))
    rows = p.shape[0]
    out_ref[:rows, :] = coded(p, k)
    out_ref[rows:, :] = jnp.broadcast_to(k, (8, 128)).astype(I32).astype(I16)


def score_kernel(p_ref, t_ref, swapped_ref, out_ref, p_all):
    nz = p_ref.shape[0]
    half = swapped_ref.shape[1]
    yh = lax.axis_index("yh")
    for z in range(nz):
        parts = []
        for c in range(2):
            v = p_ref[z, c].astype(I32).astype(F32)
            parts.append((v[:256, :] * jnp.exp2(v[256:257, :])).reshape(32, 8, 128))
        p_all[:, z * 128 : (z + 1) * 128] = (
            jnp.concatenate(parts, axis=1).reshape(512, 128).astype(BF16)
        )
    own = t_ref[:, pl.ds(pl.multiple_of(yh * half, half), half)]
    for t, at in ((own, yh), (swapped_ref[...], 1 - yh)):
        s = lax.dot_general(p_all[...], t, NT, preferred_element_type=F32).astype(BF16)
        for m in range(8):
            out_ref[m, at] = s[m * 64 : (m + 1) * 64, :]


def grant(mib):
    return pltpu.CompilerParams(vmem_limit_bytes=mib << 20)


def swap(x, axis):
    return lax.ppermute(x, axis, [(0, 1), (1, 0)])


def body(token_factors, query_tokens, fisher_inverse, train_grads):
    fisher = fisher_inverse[0]
    stored = train_grads[0]
    examples, grad = stored.shape
    half = grad // 2
    vm = pl.BlockSpec(memory_space=VMEM)

    tokens = pl.pallas_call(
        encode_kernel,
        out_shape=jax.ShapeDtypeStruct((136, 128), I16),
        in_specs=[pl.BlockSpec(memory_space=pltpu.SMEM), vm],
        out_specs=vm,
        scratch_shapes=[VMEM((128, 128), F32)],
        compiler_params=grant(ENCODE_MIB),
    )(query_tokens, token_factors[0])
    away = swap(tokens, "yh")
    fisher_other = swap(fisher, "c")
    swapped = pl.pallas_call(
        half_kernel,
        out_shape=jax.ShapeDtypeStruct((examples, half), BF16),
        in_specs=[vm, pl.BlockSpec(memory_space=pl.ANY)],
        out_specs=vm,
        compiler_params=grant(8),
    )(stored, tokens)
    swapped = swap(swapped, "yh")
    tokens = lax.all_gather(jnp.concatenate([tokens, away]), "z").reshape(16, 2, 136, 128)

    conditioned = pl.pallas_call(
        condition_kernel,
        out_shape=jax.ShapeDtypeStruct((264, 128), I16),
        in_specs=[vm, vm, vm],
        out_specs=vm,
        scratch_shapes=[VMEM((256, grad), F32), VMEM((UNROLL, 2, 64, 128), F32)],
        compiler_params=grant(24),
    )(tokens, fisher, fisher_other)
    conditioned = lax.all_gather(conditioned, ("z", "c")).reshape(16, 2, 264, 128)

    partial = pl.pallas_call(
        score_kernel,
        out_shape=jax.ShapeDtypeStruct((8, 2, 64, examples), BF16),
        in_specs=[vm, vm, vm],
        out_specs=vm,
        scratch_shapes=[VMEM((512, half), BF16)],
        compiler_params=grant(24),
    )(conditioned, stored, swapped)
    partial = lax.all_to_all(
        partial.reshape(16, 64, examples), ("x", "yl", "yh"), 0, 0, tiled=True
    )
    return jnp.sum(partial.astype(F32), axis=0).T


def solution(mesh):
    fine = Mesh(mesh.devices.reshape(4, 2, 2, 16, 2), AXES)
    module, store = ("x", "yl"), ("yh", "z", "c")
    return jax.shard_map(
        body,
        mesh=fine,
        in_specs=(
            P(module, store, None),
            P(store, None),
            P(module, store, None),
            P(module, store, None),
        ),
        out_specs=P(store, module),
        check_vma=False,
    )
```

```python
import functools

import jax
import jax.numpy as jnp
from jax import lax
from jax.experimental import pallas as pl
from jax.experimental.pallas import tpu as pltpu
from jax.sharding import Mesh, PartitionSpec as P

AXES = ("x", "yl", "yh", "z", "c")
F32, BF16, I32, I16 = jnp.float32, jnp.bfloat16, jnp.int32, jnp.int16
NT = (((1,), (1,)), ((), ()))
VMEM = pltpu.VMEM
UNROLL = 8
ENCODE_MIB = 60
HALF_MIB = 52


def exponent(largest):
    return jnp.floor(jnp.log2(jnp.maximum(largest, 1e-30))) - 13.0


def coded(x, k):
    return jnp.round(x * jnp.exp2(-k)).astype(I32).astype(I16)


def split(x):
    hi = x.astype(BF16)
    return hi, (x - hi.astype(F32)).astype(BF16)


def encode_kernel(counts_ref, tok_ref, out_ref, buf):
    buf[...] = tok_ref[...].T
    rank = buf.shape[0] // 2
    ins = buf[:rank, :]
    ogs = buf[rank:, :]
    k_in = exponent(jnp.max(jnp.abs(ins), axis=0, keepdims=True))
    k_og = exponent(jnp.max(jnp.abs(ogs), axis=0, keepdims=True))
    t = lax.broadcasted_iota(I32, (1, buf.shape[1]), 1)
    owner = jnp.zeros_like(t)
    end = 0
    for j in range(7):
        end = end + counts_ref[0, j]
        owner = owner + (t >= end).astype(I32)
    even = buf[pl.ds(rank, rank // 2, stride=2), :]
    odd = buf[pl.ds(rank + 1, rank // 2, stride=2), :]
    row = lax.broadcasted_iota(I32, (8, buf.shape[1]), 0)
    extra = jnp.where(row == 0, k_in, jnp.where(row == 1, k_og, owner.astype(F32)))
    out_ref[:rank, :] = coded(ins, k_in)
    out_ref[rank : rank + rank // 2, :] = coded(even, k_og)
    out_ref[rank + rank // 2 : 2 * rank, :] = coded(odd, k_og)
    out_ref[2 * rank :, :] = extra.astype(I32).astype(I16)


def half_kernel(t_ref, tokens_ref, half_ref, sem):
    half = half_ref.shape[1]
    at = pl.multiple_of((1 - lax.axis_index("yh")) * half, half)
    copy = pltpu.make_async_copy(t_ref.at[:, pl.ds(at, half)], half_ref, sem)
    copy.start()
    copy.wait()


def condition_kernel(tok_ref, mine_ref, other_ref, out_ref, grads, wide):
    nz = tok_ref.shape[0]
    core = lax.axis_index("c")
    j = lax.broadcasted_iota(I32, (8, 128), 0).astype(F32)

    def block(z, yh, slot):
        x = tok_ref[z, yh].astype(I32).astype(F32)
        mask = jnp.where(x[130:131, :] == j, 1.0, 0.0)
        in_hi, in_lo = split(x[0:64, :] * jnp.exp2(x[128:129, :]))
        zero = jnp.zeros((64, 128), BF16)

        def diagonal(v):
            return jnp.concatenate(
                [jnp.concatenate([v, zero], axis=1), jnp.concatenate([zero, v], axis=1)], axis=0
            )

        r_hi, r_lo = diagonal(in_hi), diagonal(in_lo)
        w = x[64:128, :] * jnp.exp2(x[129:130, :])
        hi = w.astype(BF16).astype(F32)
        wide[slot, 0] = hi
        wide[slot, 1] = w - hi

        def spread(part):
            halves = []
            for odd in range(2):
                rows = [
                    wide[slot, part, pl.ds(odd * 32 + a, 8, stride=0), :] * mask
                    for a in range(32)
                ]
                halves.append(jnp.concatenate(rows, axis=0).astype(BF16))
            return jnp.concatenate(halves, axis=1)

        two = lax.dot_general(
            spread(0), jnp.concatenate([r_hi, r_lo], axis=0), NT, preferred_element_type=F32
        )
        one = lax.dot_general(spread(1), r_hi, NT, preferred_element_type=F32)
        g = two[:, :128] + two[:, 128:] + one
        at = pl.multiple_of((yh * nz + z) * 8, 8)
        for a in range(32):
            grads[pl.ds(at, 8), a * 128 : (a + 1) * 128] = g[a * 8 : (a + 1) * 8, :]

    def step(s, carry):
        for i in range(UNROLL):
            block(s * (UNROLL // 2) + i // 2, i % 2, i)
        return carry

    lax.fori_loop(0, 2 * nz // UNROLL, step, 0)
    dot = functools.partial(lax.dot_general, dimension_numbers=NT, preferred_element_type=F32)
    wide_rows, width = mine_ref.shape[0], 512
    p = jnp.zeros((grads.shape[0], 2 * wide_rows), F32)
    for at in range(0, grads.shape[1], width):
        columns = slice(at, at + width)
        g_hi, g_lo = split(grads[:, columns])
        f = jnp.concatenate([mine_ref[:, columns], other_ref[:, columns]], axis=0)
        f_hi, f_lo = split(f)
        two = dot(g_hi, jnp.concatenate([f_hi, f_lo], axis=0))
        one = dot(g_lo, f_hi)
        p = p + (two[:, : 2 * wide_rows] + two[:, 2 * wide_rows :] + one)
    p = jnp.where(core == 0, p, pltpu.roll(p, wide_rows, 1))
    k = exponent(jnp.max(jnp.abs(p), axis=0, keepdims=True))
    rows = p.shape[0]
    out_ref[:rows, :] = coded(p, k)
    out_ref[rows:, :] = jnp.broadcast_to(k, (8, 128)).astype(I32).astype(I16)


def score_kernel(p_ref, t_ref, swapped_ref, out_ref, p_all):
    nz = p_ref.shape[0]
    half = swapped_ref.shape[1]
    yh = lax.axis_index("yh")
    for z in range(nz):
        parts = []
        for c in range(2):
            v = p_ref[z, c].astype(I32).astype(F32)
            parts.append((v[:256, :] * jnp.exp2(v[256:257, :])).reshape(32, 8, 128))
        p_all[:, z * 128 : (z + 1) * 128] = (
            jnp.concatenate(parts, axis=1).reshape(512, 128).astype(BF16)
        )
    own = t_ref[:, pl.ds(pl.multiple_of(yh * half, half), half)]
    for t, at in ((own, yh), (swapped_ref[...], 1 - yh)):
        s = lax.dot_general(p_all[...], t, NT, preferred_element_type=F32).astype(BF16)
        for m in range(8):
            out_ref[m, at] = s[m * 64 : (m + 1) * 64, :]


def grant(mib):
    return pltpu.CompilerParams(vmem_limit_bytes=mib << 20)


def swap(x, axis):
    return lax.ppermute(x, axis, [(0, 1), (1, 0)])


def body(token_factors, query_tokens, fisher_inverse, train_grads):
    fisher = fisher_inverse[0]
    stored = train_grads[0]
    examples, grad = stored.shape
    half = grad // 2
    vm = pl.BlockSpec(memory_space=VMEM)

    tokens = pl.pallas_call(
        encode_kernel,
        out_shape=jax.ShapeDtypeStruct((136, 128), I16),
        in_specs=[pl.BlockSpec(memory_space=pltpu.SMEM), vm],
        out_specs=vm,
        scratch_shapes=[VMEM((128, 128), F32)],
        compiler_params=grant(ENCODE_MIB),
    )(query_tokens, token_factors[0])
    tokens = lax.all_gather(tokens, "yh")
    fisher_other = swap(fisher, "c")
    swapped = pl.pallas_call(
        half_kernel,
        out_shape=jax.ShapeDtypeStruct((examples, half), BF16),
        in_specs=[pl.BlockSpec(memory_space=pl.ANY), vm],
        out_specs=vm,
        scratch_shapes=[pltpu.SemaphoreType.DMA],
        compiler_params=grant(HALF_MIB),
    )(stored, tokens)
    swapped = swap(swapped, "yh")
    tokens = lax.all_gather(tokens, "z").reshape(16, 2, 136, 128)

    conditioned = pl.pallas_call(
        condition_kernel,
        out_shape=jax.ShapeDtypeStruct((264, 128), I16),
        in_specs=[vm, vm, vm],
        out_specs=vm,
        scratch_shapes=[VMEM((256, grad), F32), VMEM((UNROLL, 2, 64, 128), F32)],
        compiler_params=grant(24),
    )(tokens, fisher, fisher_other)
    conditioned = lax.all_gather(conditioned, ("z", "c")).reshape(16, 2, 264, 128)

    partial = pl.pallas_call(
        score_kernel,
        out_shape=jax.ShapeDtypeStruct((8, 2, 64, examples), BF16),
        in_specs=[vm, vm, vm],
        out_specs=vm,
        scratch_shapes=[VMEM((512, half), BF16)],
        compiler_params=grant(24),
    )(conditioned, stored, swapped)
    partial = lax.all_to_all(
        partial.reshape(16, 64, examples), ("x", "yl", "yh"), 0, 0, tiled=True
    )
    return jnp.sum(partial.astype(F32), axis=0).T


def solution(mesh):
    fine = Mesh(mesh.devices.reshape(4, 2, 2, 16, 2), AXES)
    module, store = ("x", "yl"), ("yh", "z", "c")
    return jax.shard_map(
        body,
        mesh=fine,
        in_specs=(
            P(module, store, None),
            P(store, None),
            P(module, store, None),
            P(module, store, None),
        ),
        out_specs=P(store, module),
        check_vma=False,
    )
```

```python
import functools

import jax
import jax.numpy as jnp
from jax import lax
from jax.experimental import pallas as pl
from jax.experimental.pallas import tpu as pltpu
from jax.sharding import Mesh, PartitionSpec as P

AXES = ("x", "yl", "yh", "z", "c")
F32, BF16, I32, I16 = jnp.float32, jnp.bfloat16, jnp.int32, jnp.int16
NT = (((1,), (1,)), ((), ()))
VMEM = pltpu.VMEM
UNROLL = 8
ENCODE_MIB = 60


def exponent(largest):
    return jnp.floor(jnp.log2(jnp.maximum(largest, 1e-30))) - 13.0


def coded(x, k):
    return jnp.round(x * jnp.exp2(-k)).astype(I32).astype(I16)


def split(x):
    hi = x.astype(BF16)
    return hi, (x - hi.astype(F32)).astype(BF16)


def encode_kernel(counts_ref, tok_ref, out_ref, buf):
    buf[...] = tok_ref[...].T
    rank = buf.shape[0] // 2
    ins = buf[:rank, :]
    ogs = buf[rank:, :]
    k_in = exponent(jnp.max(jnp.abs(ins), axis=0, keepdims=True))
    k_og = exponent(jnp.max(jnp.abs(ogs), axis=0, keepdims=True))
    t = lax.broadcasted_iota(I32, (1, buf.shape[1]), 1)
    owner = jnp.zeros_like(t)
    end = 0
    for j in range(7):
        end = end + counts_ref[0, j]
        owner = owner + (t >= end).astype(I32)
    even = buf[pl.ds(rank, rank // 2, stride=2), :]
    odd = buf[pl.ds(rank + 1, rank // 2, stride=2), :]
    row = lax.broadcasted_iota(I32, (8, buf.shape[1]), 0)
    extra = jnp.where(row == 0, k_in, jnp.where(row == 1, k_og, owner.astype(F32)))
    out_ref[:rank, :] = coded(ins, k_in)
    out_ref[rank : rank + rank // 2, :] = coded(even, k_og)
    out_ref[rank + rank // 2 : 2 * rank, :] = coded(odd, k_og)
    out_ref[2 * rank :, :] = extra.astype(I32).astype(I16)


def condition_kernel(tok_ref, mine_ref, other_ref, out_ref, grads, wide):
    nz, nc = tok_ref.shape[:2]
    j = lax.broadcasted_iota(I32, (8, 128), 0).astype(F32)

    def block(z, c, slot):
        x = tok_ref[z, c].astype(I32).astype(F32)
        mask = jnp.where(x[130:131, :] == j, 1.0, 0.0)
        in_hi, in_lo = split(x[0:64, :] * jnp.exp2(x[128:129, :]))
        zero = jnp.zeros((64, 128), BF16)

        def diagonal(v):
            return jnp.concatenate(
                [jnp.concatenate([v, zero], axis=1), jnp.concatenate([zero, v], axis=1)], axis=0
            )

        r_hi, r_lo = diagonal(in_hi), diagonal(in_lo)
        w = x[64:128, :] * jnp.exp2(x[129:130, :])
        hi = w.astype(BF16).astype(F32)
        wide[slot, 0] = hi
        wide[slot, 1] = w - hi

        def spread(part):
            halves = []
            for odd in range(2):
                rows = [
                    wide[slot, part, pl.ds(odd * 32 + a, 8, stride=0), :] * mask
                    for a in range(32)
                ]
                halves.append(jnp.concatenate(rows, axis=0).astype(BF16))
            return jnp.concatenate(halves, axis=1)

        two = lax.dot_general(
            spread(0), jnp.concatenate([r_hi, r_lo], axis=0), NT, preferred_element_type=F32
        )
        one = lax.dot_general(spread(1), r_hi, NT, preferred_element_type=F32)
        g = two[:, :128] + two[:, 128:] + one
        at = pl.multiple_of((z * nc + c) * 8, 8)
        for a in range(32):
            grads[pl.ds(at, 8), a * 128 : (a + 1) * 128] = g[a * 8 : (a + 1) * 8, :]

    def step(s, carry):
        for i in range(UNROLL):
            block(s * (UNROLL // 2) + i // 2, i % 2, i)
        return carry

    lax.fori_loop(0, nc * nz // UNROLL, step, 0)
    dot = functools.partial(lax.dot_general, dimension_numbers=NT, preferred_element_type=F32)
    wide_rows, width = mine_ref.shape[0], 512
    p = jnp.zeros((grads.shape[0], 2 * wide_rows), F32)
    for at in range(0, grads.shape[1], width):
        columns = slice(at, at + width)
        g_hi, g_lo = split(grads[:, columns])
        f = jnp.concatenate([mine_ref[:, columns], other_ref[:, columns]], axis=0)
        f_hi, f_lo = split(f)
        two = dot(g_hi, jnp.concatenate([f_hi, f_lo], axis=0))
        one = dot(g_lo, f_hi)
        p = p + (two[:, : 2 * wide_rows] + two[:, 2 * wide_rows :] + one)
    p = jnp.where(lax.axis_index("c") == lax.axis_index("yh"), p, pltpu.roll(p, wide_rows, 1))
    k = exponent(jnp.max(jnp.abs(p), axis=0, keepdims=True))
    rows = p.shape[0]
    out_ref[:rows, :] = coded(p, k)
    out_ref[rows:, :] = jnp.broadcast_to(k, (8, 128)).astype(I32).astype(I16)


def score_kernel(p_ref, t_ref, out_ref, p_all):
    nz, _, ny, rows, lanes = p_ref.shape
    rows = rows - 8
    first = lax.broadcasted_iota(I32, (rows, lanes), 1) < lanes // 2
    for z in range(nz):
        for yh in range(ny):
            v = [p_ref[z, c, yh].astype(I32).astype(F32) for c in range(2)]
            v = [u[:rows, :] * jnp.exp2(u[rows : rows + 1, :]) for u in v]
            low = jnp.where(first, v[0], v[1])
            high = pltpu.roll(jnp.where(first, v[1], v[0]), lanes // 2, 1)
            for half, tile in ((0, low), (1, high)):
                at = (half * nz + z) * lanes
                p_all[yh * rows : (yh + 1) * rows, at : at + lanes] = tile.astype(BF16)
    s = lax.dot_general(p_all[...], t_ref[...], NT, preferred_element_type=F32).astype(BF16)
    for m in range(8):
        out_ref[m] = s[m * 64 : (m + 1) * 64, :]


def grant(mib):
    return pltpu.CompilerParams(vmem_limit_bytes=mib << 20)


def swap(x, axis):
    return lax.ppermute(x, axis, [(0, 1), (1, 0)])


def body(token_factors, query_tokens, fisher_inverse, train_grads):
    fisher = fisher_inverse[0]
    stored = train_grads[0]
    examples, grad = stored.shape
    vm = pl.BlockSpec(memory_space=VMEM)

    tokens = pl.pallas_call(
        encode_kernel,
        out_shape=jax.ShapeDtypeStruct((136, 128), I16),
        in_specs=[pl.BlockSpec(memory_space=pltpu.SMEM), vm],
        out_specs=vm,
        scratch_shapes=[VMEM((128, 128), F32)],
        compiler_params=grant(ENCODE_MIB),
    )(query_tokens, token_factors[0])
    fisher_other = swap(fisher, "yh")
    tokens = lax.all_gather(tokens, ("z", "c")).reshape(16, 2, 136, 128)

    conditioned = pl.pallas_call(
        condition_kernel,
        out_shape=jax.ShapeDtypeStruct((264, 128), I16),
        in_specs=[vm, vm, vm],
        out_specs=vm,
        scratch_shapes=[VMEM((256, grad), F32), VMEM((UNROLL, 2, 64, 128), F32)],
        compiler_params=grant(24),
    )(tokens, fisher, fisher_other)
    conditioned = lax.all_gather(conditioned, "yh")
    conditioned = lax.all_gather(conditioned, ("z", "c")).reshape(16, 2, 2, 264, 128)

    partial = pl.pallas_call(
        score_kernel,
        out_shape=jax.ShapeDtypeStruct((8, 64, examples), BF16),
        in_specs=[vm, vm],
        out_specs=vm,
        scratch_shapes=[VMEM((512, grad), BF16)],
        compiler_params=grant(24),
    )(conditioned, stored)
    partial = lax.all_to_all(partial, ("x", "yl"), 0, 0, tiled=True)
    return jnp.sum(partial.astype(F32), axis=0).T


def solution(mesh):
    fine = Mesh(mesh.devices.reshape(4, 2, 2, 16, 2), AXES)
    module, store = ("x", "yl"), ("yh", "z", "c")
    return jax.shard_map(
        body,
        mesh=fine,
        in_specs=(
            P(module, store, None),
            P(store, None),
            P(module, store, None),
            P(module, store, None),
        ),
        out_specs=P(store, module),
        check_vma=False,
    )
```

```python
import functools

import jax
import jax.numpy as jnp
from jax import lax
from jax.experimental import pallas as pl
from jax.experimental.pallas import tpu as pltpu
from jax.sharding import Mesh, PartitionSpec as P

AXES = ("x", "yl", "yh", "z", "c")
F32, BF16, I32, I16 = jnp.float32, jnp.bfloat16, jnp.int32, jnp.int16
NT = (((1,), (1,)), ((), ()))
VMEM = pltpu.VMEM
UNROLL = 8
ENCODE_MIB = 8


def exponent(largest):
    return jnp.floor(jnp.log2(jnp.maximum(largest, 1e-30))) - 13.0


def coded(x, k):
    return jnp.round(x * jnp.exp2(-k)).astype(I32).astype(I16)


def split(x):
    hi = x.astype(BF16)
    return hi, (x - hi.astype(F32)).astype(BF16)


def encode_kernel(counts_ref, tok_ref, out_ref, buf):
    buf[...] = tok_ref[...].T
    rank = buf.shape[0] // 2
    ins = buf[:rank, :]
    ogs = buf[rank:, :]
    k_in = exponent(jnp.max(jnp.abs(ins), axis=0, keepdims=True))
    k_og = exponent(jnp.max(jnp.abs(ogs), axis=0, keepdims=True))
    t = lax.broadcasted_iota(I32, (1, buf.shape[1]), 1)
    owner = jnp.zeros_like(t)
    end = 0
    for j in range(7):
        end = end + counts_ref[0, j]
        owner = owner + (t >= end).astype(I32)
    even = buf[pl.ds(rank, rank // 2, stride=2), :]
    odd = buf[pl.ds(rank + 1, rank // 2, stride=2), :]
    row = lax.broadcasted_iota(I32, (8, buf.shape[1]), 0)
    extra = jnp.where(row == 0, k_in, jnp.where(row == 1, k_og, owner.astype(F32)))
    out_ref[:rank, :] = coded(ins, k_in)
    out_ref[rank : rank + rank // 2, :] = coded(even, k_og)
    out_ref[rank + rank // 2 : 2 * rank, :] = coded(odd, k_og)
    out_ref[2 * rank :, :] = extra.astype(I32).astype(I16)


def condition_kernel(tok_ref, rows_ref, other_ref, out_ref, grads, wide, mine_ref, sem):
    load = pltpu.make_async_copy(rows_ref, mine_ref, sem)
    load.start()
    nz, nc = tok_ref.shape[:2]
    j = lax.broadcasted_iota(I32, (8, 128), 0).astype(F32)

    def block(z, c, slot):
        x = tok_ref[z, c].astype(I32).astype(F32)
        mask = jnp.where(x[130:131, :] == j, 1.0, 0.0)
        in_hi, in_lo = split(x[0:64, :] * jnp.exp2(x[128:129, :]))
        zero = jnp.zeros((64, 128), BF16)

        def diagonal(v):
            return jnp.concatenate(
                [jnp.concatenate([v, zero], axis=1), jnp.concatenate([zero, v], axis=1)], axis=0
            )

        r_hi, r_lo = diagonal(in_hi), diagonal(in_lo)
        w = x[64:128, :] * jnp.exp2(x[129:130, :])
        hi = w.astype(BF16).astype(F32)
        wide[slot, 0] = hi
        wide[slot, 1] = w - hi

        def spread(part):
            halves = []
            for odd in range(2):
                rows = [
                    wide[slot, part, pl.ds(odd * 32 + a, 8, stride=0), :] * mask
                    for a in range(32)
                ]
                halves.append(jnp.concatenate(rows, axis=0).astype(BF16))
            return jnp.concatenate(halves, axis=1)

        two = lax.dot_general(
            spread(0), jnp.concatenate([r_hi, r_lo], axis=0), NT, preferred_element_type=F32
        )
        one = lax.dot_general(spread(1), r_hi, NT, preferred_element_type=F32)
        g = two[:, :128] + two[:, 128:] + one
        at = pl.multiple_of((z * nc + c) * 8, 8)
        for a in range(32):
            grads[pl.ds(at, 8), a * 128 : (a + 1) * 128] = g[a * 8 : (a + 1) * 8, :]

    def step(s, carry):
        for i in range(UNROLL):
            block(s * (UNROLL // 2) + i // 2, i % 2, i)
        return carry

    lax.fori_loop(0, nc * nz // UNROLL, step, 0)
    dot = functools.partial(lax.dot_general, dimension_numbers=NT, preferred_element_type=F32)
    load.wait()
    wide_rows, width = mine_ref.shape[0], 512
    p = jnp.zeros((grads.shape[0], 2 * wide_rows), F32)
    for at in range(0, grads.shape[1], width):
        columns = slice(at, at + width)
        g_hi, g_lo = split(grads[:, columns])
        f = jnp.concatenate([mine_ref[:, columns], other_ref[:, columns]], axis=0)
        f_hi, f_lo = split(f)
        two = dot(g_hi, jnp.concatenate([f_hi, f_lo], axis=0))
        one = dot(g_lo, f_hi)
        p = p + (two[:, : 2 * wide_rows] + two[:, 2 * wide_rows :] + one)
    p = jnp.where(lax.axis_index("c") == lax.axis_index("yh"), p, pltpu.roll(p, wide_rows, 1))
    k = exponent(jnp.max(jnp.abs(p), axis=0, keepdims=True))
    rows = p.shape[0]
    out_ref[:rows, :] = coded(p, k)
    out_ref[rows:, :] = jnp.broadcast_to(k, (8, 128)).astype(I32).astype(I16)


def score_kernel(p_ref, t_ref, out_ref, p_all):
    nz, _, ny, rows, lanes = p_ref.shape
    rows = rows - 8
    first = lax.broadcasted_iota(I32, (rows, lanes), 1) < lanes // 2
    for z in range(nz):
        for yh in range(ny):
            v = [p_ref[z, c, yh].astype(I32).astype(F32) for c in range(2)]
            v = [u[:rows, :] * jnp.exp2(u[rows : rows + 1, :]) for u in v]
            low = jnp.where(first, v[0], v[1])
            high = pltpu.roll(jnp.where(first, v[1], v[0]), lanes // 2, 1)
            for half, tile in ((0, low), (1, high)):
                at = (half * nz + z) * lanes
                p_all[yh * rows : (yh + 1) * rows, at : at + lanes] = tile.astype(BF16)
    s = lax.dot_general(p_all[...], t_ref[...], NT, preferred_element_type=F32).astype(BF16)
    for m in range(8):
        out_ref[m] = s[m * 64 : (m + 1) * 64, :]


def grant(mib):
    return pltpu.CompilerParams(vmem_limit_bytes=mib << 20)


def in_hbm(x):
    return pltpu.with_memory_space_constraint(x, pltpu.HBM)


def swap(x, axis):
    return lax.ppermute(x, axis, [(0, 1), (1, 0)])


def body(token_factors, query_tokens, fisher_inverse, train_grads):
    fisher = fisher_inverse[0]
    stored = train_grads[0]
    examples, grad = stored.shape
    vm = pl.BlockSpec(memory_space=VMEM)

    tokens = pl.pallas_call(
        encode_kernel,
        out_shape=pltpu.VMEM((136, 128), I16),
        in_specs=[pl.BlockSpec(memory_space=pltpu.SMEM), vm],
        out_specs=vm,
        scratch_shapes=[VMEM((128, 128), F32)],
        compiler_params=grant(ENCODE_MIB),
    )(in_hbm(query_tokens), in_hbm(token_factors[0]))
    fisher_other = swap(fisher, "yh")
    tokens = lax.all_gather(tokens, ("z", "c")).reshape(16, 2, 136, 128)

    conditioned = pl.pallas_call(
        condition_kernel,
        out_shape=jax.ShapeDtypeStruct((264, 128), I16),
        in_specs=[vm, pl.BlockSpec(memory_space=pl.ANY), vm],
        out_specs=vm,
        scratch_shapes=[
            VMEM((256, grad), F32),
            VMEM((UNROLL, 2, 64, 128), F32),
            VMEM(fisher.shape, F32),
            pltpu.SemaphoreType.DMA,
        ],
        compiler_params=grant(24),
    )(tokens, in_hbm(fisher), fisher_other)
    conditioned = lax.all_gather(conditioned, "yh")
    conditioned = lax.all_gather(conditioned, ("z", "c")).reshape(16, 2, 2, 264, 128)

    partial = pl.pallas_call(
        score_kernel,
        out_shape=jax.ShapeDtypeStruct((8, 64, examples), BF16),
        in_specs=[vm, vm],
        out_specs=vm,
        scratch_shapes=[VMEM((512, grad), BF16)],
        compiler_params=grant(24),
    )(conditioned, stored)
    partial = lax.all_to_all(partial, ("x", "yl"), 0, 0, tiled=True)
    return jnp.sum(partial.astype(F32), axis=0).T


def solution(mesh):
    fine = Mesh(mesh.devices.reshape(4, 2, 2, 16, 2), AXES)
    module, store = ("x", "yl"), ("yh", "z", "c")
    return jax.shard_map(
        body,
        mesh=fine,
        in_specs=(
            P(module, store, None),
            P(store, None),
            P(module, store, None),
            P(module, store, None),
        ),
        out_specs=P(store, module),
        check_vma=False,
    )
```

```python
import functools

import jax
import jax.numpy as jnp
from jax import lax
from jax.experimental import pallas as pl
from jax.experimental.pallas import tpu as pltpu
from jax.sharding import Mesh, PartitionSpec as P

AXES = ("x", "yl", "yh", "z", "c")
F32, BF16, I32, I16 = jnp.float32, jnp.bfloat16, jnp.int32, jnp.int16
NT = (((1,), (1,)), ((), ()))
VMEM = pltpu.VMEM
UNROLL = 8
ENCODE_MIB = 8


def exponent(largest):
    return jnp.floor(jnp.log2(jnp.maximum(largest, 1e-30))) - 13.0


def coded(x, k):
    return jnp.round(x * jnp.exp2(-k)).astype(I32).astype(I16)


def split(x):
    hi = x.astype(BF16)
    return hi, (x - hi.astype(F32)).astype(BF16)


def encode_kernel(counts_ref, tok_ref, out_ref, buf):
    x = tok_ref[...].T
    rank = x.shape[0] // 2
    buf[: 2 * rank, :] = x
    ins = x[:rank, :]
    ogs = x[rank:, :]
    k_in = exponent(jnp.max(jnp.abs(ins), axis=0, keepdims=True))
    k_og = exponent(jnp.max(jnp.abs(ogs), axis=0, keepdims=True))
    t = lax.broadcasted_iota(I32, (1, x.shape[1]), 1)
    owner = jnp.zeros_like(t)
    end = 0
    for j in range(7):
        end = end + counts_ref[0, j]
        owner = owner + (t >= end).astype(I32)
    even = buf[pl.ds(rank, rank // 2, stride=2), :]
    odd = buf[pl.ds(rank + 1, rank // 2, stride=2), :]
    row = lax.broadcasted_iota(I32, (8, x.shape[1]), 0)
    extra = jnp.where(row == 0, k_in, jnp.where(row == 1, k_og, owner.astype(F32)))
    out_ref[:rank, :] = coded(ins, k_in)
    out_ref[rank : rank + rank // 2, :] = coded(even, k_og)
    out_ref[rank + rank // 2 : 2 * rank, :] = coded(odd, k_og)
    out_ref[2 * rank :, :] = extra.astype(I32).astype(I16)


def condition_kernel(tok_ref, rows_ref, other_ref, out_ref, grads, wide, mine_ref, sem):
    load = pltpu.make_async_copy(rows_ref, mine_ref, sem)
    load.start()
    nz, nc = tok_ref.shape[:2]
    j = lax.broadcasted_iota(I32, (8, 128), 0).astype(F32)

    def block(z, c, slot):
        x = tok_ref[z, c].astype(I32).astype(F32)
        mask = jnp.where(x[130:131, :] == j, 1.0, 0.0)
        in_hi, in_lo = split(x[0:64, :] * jnp.exp2(x[128:129, :]))
        zero = jnp.zeros((64, 128), BF16)

        def diagonal(v):
            return jnp.concatenate(
                [jnp.concatenate([v, zero], axis=1), jnp.concatenate([zero, v], axis=1)], axis=0
            )

        r_hi, r_lo = diagonal(in_hi), diagonal(in_lo)
        w = x[64:128, :] * jnp.exp2(x[129:130, :])
        hi = w.astype(BF16).astype(F32)
        wide[slot, 0, 0:64, :] = hi
        wide[slot, 1, 0:64, :] = w - hi

        def spread(part):
            halves = []
            for odd in range(2):
                rows = [
                    wide[slot, part, pl.ds(odd * 32 + a, 8, stride=0), :] * mask
                    for a in range(32)
                ]
                halves.append(jnp.concatenate(rows, axis=0).astype(BF16))
            return jnp.concatenate(halves, axis=1)

        two = lax.dot_general(
            spread(0), jnp.concatenate([r_hi, r_lo], axis=0), NT, preferred_element_type=F32
        )
        one = lax.dot_general(spread(1), r_hi, NT, preferred_element_type=F32)
        g = two[:, :128] + two[:, 128:] + one
        at = pl.multiple_of((z * nc + c) * 8, 8)
        for a in range(32):
            grads[pl.ds(at, 8), a * 128 : (a + 1) * 128] = g[a * 8 : (a + 1) * 8, :]

    def step(s, carry):
        for i in range(UNROLL):
            block(s * (UNROLL // 2) + i // 2, i % 2, i)
        return carry

    lax.fori_loop(0, nc * nz // UNROLL, step, 0)
    dot = functools.partial(lax.dot_general, dimension_numbers=NT, preferred_element_type=F32)
    load.wait()
    wide_rows, width = mine_ref.shape[0], 512
    p = jnp.zeros((grads.shape[0], 2 * wide_rows), F32)
    for at in range(0, grads.shape[1], width):
        columns = slice(at, at + width)
        g_hi, g_lo = split(grads[:, columns])
        f = jnp.concatenate([mine_ref[:, columns], other_ref[:, columns]], axis=0)
        f_hi, f_lo = split(f)
        two = dot(g_hi, jnp.concatenate([f_hi, f_lo], axis=0))
        one = dot(g_lo, f_hi)
        p = p + (two[:, : 2 * wide_rows] + two[:, 2 * wide_rows :] + one)
    p = jnp.where(lax.axis_index("c") == lax.axis_index("yh"), p, pltpu.roll(p, wide_rows, 1))
    k = exponent(jnp.max(jnp.abs(p), axis=0, keepdims=True))
    rows = p.shape[0]
    out_ref[:rows, :] = coded(p, k)
    out_ref[rows:, :] = jnp.broadcast_to(k, (8, 128)).astype(I32).astype(I16)


def score_kernel(p_ref, t_ref, out_ref, p_all):
    nz, _, ny, rows, lanes = p_ref.shape
    rows = rows - 8
    first = lax.broadcasted_iota(I32, (rows, lanes), 1) < lanes // 2
    for z in range(nz):
        for yh in range(ny):
            v = [p_ref[z, c, yh].astype(I32).astype(F32) for c in range(2)]
            v = [u[:rows, :] * jnp.exp2(u[rows : rows + 1, :]) for u in v]
            low = jnp.where(first, v[0], v[1])
            high = pltpu.roll(jnp.where(first, v[1], v[0]), lanes // 2, 1)
            for half, tile in ((0, low), (1, high)):
                at = (half * nz + z) * lanes
                p_all[yh * rows : (yh + 1) * rows, at : at + lanes] = tile.astype(BF16)
    s = lax.dot_general(p_all[...], t_ref[...], NT, preferred_element_type=F32).astype(BF16)
    for m in range(8):
        out_ref[m] = s[m * 64 : (m + 1) * 64, :]


def grant(mib):
    return pltpu.CompilerParams(vmem_limit_bytes=mib << 20)


def in_hbm(x):
    return pltpu.with_memory_space_constraint(x, pltpu.HBM)


def swap(x, axis):
    return lax.ppermute(x, axis, [(0, 1), (1, 0)])


def body(token_factors, query_tokens, fisher_inverse, train_grads):
    fisher = fisher_inverse[0]
    stored = train_grads[0]
    examples, grad = stored.shape
    vm = pl.BlockSpec(memory_space=VMEM)

    tokens = pl.pallas_call(
        encode_kernel,
        out_shape=pltpu.VMEM((136, 128), I16),
        in_specs=[pl.BlockSpec(memory_space=pltpu.SMEM), vm],
        out_specs=vm,
        scratch_shapes=[VMEM((136, 128), F32)],
        compiler_params=grant(ENCODE_MIB),
    )(in_hbm(query_tokens), in_hbm(token_factors[0]))
    fisher_other = swap(fisher, "yh")
    tokens = lax.all_gather(tokens, ("z", "c")).reshape(16, 2, 136, 128)

    conditioned = pl.pallas_call(
        condition_kernel,
        out_shape=jax.ShapeDtypeStruct((264, 128), I16),
        in_specs=[vm, pl.BlockSpec(memory_space=pl.ANY), vm],
        out_specs=vm,
        scratch_shapes=[
            VMEM((256, grad), F32),
            VMEM((UNROLL, 2, 72, 128), F32),
            VMEM(fisher.shape, F32),
            pltpu.SemaphoreType.DMA,
        ],
        compiler_params=grant(24),
    )(tokens, in_hbm(fisher), fisher_other)
    conditioned = lax.all_gather(conditioned, "yh")
    conditioned = lax.all_gather(conditioned, ("z", "c")).reshape(16, 2, 2, 264, 128)

    partial = pl.pallas_call(
        score_kernel,
        out_shape=jax.ShapeDtypeStruct((8, 64, examples), BF16),
        in_specs=[vm, vm],
        out_specs=vm,
        scratch_shapes=[VMEM((512, grad), BF16)],
        compiler_params=grant(24),
    )(conditioned, stored)
    partial = lax.all_to_all(partial, ("x", "yl"), 0, 0, tiled=True)
    return jnp.sum(partial.astype(F32), axis=0).T


def solution(mesh):
    fine = Mesh(mesh.devices.reshape(4, 2, 2, 16, 2), AXES)
    module, store = ("x", "yl"), ("yh", "z", "c")
    return jax.shard_map(
        body,
        mesh=fine,
        in_specs=(
            P(module, store, None),
            P(store, None),
            P(module, store, None),
            P(module, store, None),
        ),
        out_specs=P(store, module),
        check_vma=False,
    )
```

```python
import functools

import jax
import jax.numpy as jnp
from jax import lax
from jax.experimental import pallas as pl
from jax.experimental.pallas import tpu as pltpu
from jax.sharding import Mesh, PartitionSpec as P

AXES = ("x", "yl", "yh", "z", "c")
F32, BF16, I32, I16 = jnp.float32, jnp.bfloat16, jnp.int32, jnp.int16
NT = (((1,), (1,)), ((), ()))
VMEM = pltpu.VMEM
UNROLL = 16
ENCODE_MIB = 8


def exponent(largest):
    return jnp.floor(jnp.log2(jnp.maximum(largest, 1e-30))) - 13.0


def coded(x, k):
    return jnp.round(x * jnp.exp2(-k)).astype(I32).astype(I16)


def split(x):
    hi = x.astype(BF16)
    return hi, (x - hi.astype(F32)).astype(BF16)


def encode_kernel(counts_ref, tok_ref, out_ref, buf):
    x = tok_ref[...].T
    rank = x.shape[0] // 2
    buf[: 2 * rank, :] = x
    ins = x[:rank, :]
    ogs = x[rank:, :]
    k_in = exponent(jnp.max(jnp.abs(ins), axis=0, keepdims=True))
    k_og = exponent(jnp.max(jnp.abs(ogs), axis=0, keepdims=True))
    t = lax.broadcasted_iota(I32, (1, x.shape[1]), 1)
    owner = jnp.zeros_like(t)
    end = 0
    for j in range(7):
        end = end + counts_ref[0, j]
        owner = owner + (t >= end).astype(I32)
    even = buf[pl.ds(rank, rank // 2, stride=2), :]
    odd = buf[pl.ds(rank + 1, rank // 2, stride=2), :]
    row = lax.broadcasted_iota(I32, (8, x.shape[1]), 0)
    extra = jnp.where(row == 0, k_in, jnp.where(row == 1, k_og, owner.astype(F32)))
    out_ref[:rank, :] = coded(ins, k_in)
    out_ref[rank : rank + rank // 2, :] = coded(even, k_og)
    out_ref[rank + rank // 2 : 2 * rank, :] = coded(odd, k_og)
    out_ref[2 * rank :, :] = extra.astype(I32).astype(I16)


def condition_kernel(tok_ref, rows_ref, other_ref, out_ref, grads, wide, mine_ref, sem):
    load = pltpu.make_async_copy(rows_ref, mine_ref, sem)
    load.start()
    nz, nc = tok_ref.shape[:2]
    j = lax.broadcasted_iota(I32, (8, 128), 0).astype(F32)

    def block(z, c, slot):
        x = tok_ref[z, c].astype(I32).astype(F32)
        mask = jnp.where(x[130:131, :] == j, 1.0, 0.0)
        in_hi, in_lo = split(x[0:64, :] * jnp.exp2(x[128:129, :]))
        zero = jnp.zeros((64, 128), BF16)

        def diagonal(v):
            return jnp.concatenate(
                [jnp.concatenate([v, zero], axis=1), jnp.concatenate([zero, v], axis=1)], axis=0
            )

        r_hi, r_lo = diagonal(in_hi), diagonal(in_lo)
        w = x[64:128, :] * jnp.exp2(x[129:130, :])
        hi = w.astype(BF16).astype(F32)
        wide[slot, 0, 0:64, :] = hi
        wide[slot, 1, 0:64, :] = w - hi

        def spread(part):
            halves = []
            for odd in range(2):
                rows = [
                    wide[slot, part, pl.ds(odd * 32 + a, 8, stride=0), :] * mask
                    for a in range(32)
                ]
                halves.append(jnp.concatenate(rows, axis=0).astype(BF16))
            return jnp.concatenate(halves, axis=1)

        two = lax.dot_general(
            spread(0), jnp.concatenate([r_hi, r_lo], axis=0), NT, preferred_element_type=F32
        )
        one = lax.dot_general(spread(1), r_hi, NT, preferred_element_type=F32)
        g = two[:, :128] + two[:, 128:] + one
        at = pl.multiple_of((z * nc + c) * 8, 8)
        for a in range(32):
            grads[pl.ds(at, 8), a * 128 : (a + 1) * 128] = g[a * 8 : (a + 1) * 8, :]

    def step(s, carry):
        for i in range(UNROLL):
            block(s * (UNROLL // 2) + i // 2, i % 2, i)
        return carry

    lax.fori_loop(0, nc * nz // UNROLL, step, 0)
    dot = functools.partial(lax.dot_general, dimension_numbers=NT, preferred_element_type=F32)
    load.wait()
    wide_rows, width = mine_ref.shape[0], 512
    p = jnp.zeros((grads.shape[0], 2 * wide_rows), F32)
    for at in range(0, grads.shape[1], width):
        columns = slice(at, at + width)
        g_hi, g_lo = split(grads[:, columns])
        f = jnp.concatenate([mine_ref[:, columns], other_ref[:, columns]], axis=0)
        f_hi, f_lo = split(f)
        two = dot(g_hi, jnp.concatenate([f_hi, f_lo], axis=0))
        one = dot(g_lo, f_hi)
        p = p + (two[:, : 2 * wide_rows] + two[:, 2 * wide_rows :] + one)
    p = jnp.where(lax.axis_index("c") == lax.axis_index("yh"), p, pltpu.roll(p, wide_rows, 1))
    k = exponent(jnp.max(jnp.abs(p), axis=0, keepdims=True))
    rows = p.shape[0]
    out_ref[:rows, :] = coded(p, k)
    out_ref[rows:, :] = jnp.broadcast_to(k, (8, 128)).astype(I32).astype(I16)


def score_kernel(p_ref, t_ref, out_ref, p_all):
    nz, _, ny, rows, lanes = p_ref.shape
    rows = rows - 8
    first = lax.broadcasted_iota(I32, (rows, lanes), 1) < lanes // 2
    for z in range(nz):
        for yh in range(ny):
            v = [p_ref[z, c, yh].astype(I32).astype(F32) for c in range(2)]
            v = [u[:rows, :] * jnp.exp2(u[rows : rows + 1, :]) for u in v]
            low = jnp.where(first, v[0], v[1])
            high = pltpu.roll(jnp.where(first, v[1], v[0]), lanes // 2, 1)
            for half, tile in ((0, low), (1, high)):
                at = (half * nz + z) * lanes
                p_all[yh * rows : (yh + 1) * rows, at : at + lanes] = tile.astype(BF16)
    s = lax.dot_general(t_ref[...], p_all[...], NT, preferred_element_type=F32).T.astype(BF16)
    for m in range(8):
        out_ref[m] = s[m * 64 : (m + 1) * 64, :]


def grant(mib):
    return pltpu.CompilerParams(vmem_limit_bytes=mib << 20)


def in_hbm(x):
    return pltpu.with_memory_space_constraint(x, pltpu.HBM)


def swap(x, axis):
    return lax.ppermute(x, axis, [(0, 1), (1, 0)])


def body(token_factors, query_tokens, fisher_inverse, train_grads):
    fisher = fisher_inverse[0]
    stored = train_grads[0]
    examples, grad = stored.shape
    vm = pl.BlockSpec(memory_space=VMEM)

    tokens = pl.pallas_call(
        encode_kernel,
        out_shape=pltpu.VMEM((136, 128), I16),
        in_specs=[pl.BlockSpec(memory_space=pltpu.SMEM), vm],
        out_specs=vm,
        scratch_shapes=[VMEM((136, 128), F32)],
        compiler_params=grant(ENCODE_MIB),
    )(in_hbm(query_tokens), in_hbm(token_factors[0]))
    fisher_other = swap(fisher, "yh")
    tokens = lax.all_gather(tokens, ("z", "c")).reshape(16, 2, 136, 128)

    conditioned = pl.pallas_call(
        condition_kernel,
        out_shape=jax.ShapeDtypeStruct((264, 128), I16),
        in_specs=[vm, pl.BlockSpec(memory_space=pl.ANY), vm],
        out_specs=vm,
        scratch_shapes=[
            VMEM((256, grad), F32),
            VMEM((UNROLL, 2, 72, 128), F32),
            VMEM(fisher.shape, F32),
            pltpu.SemaphoreType.DMA,
        ],
        compiler_params=grant(24),
    )(tokens, in_hbm(fisher), fisher_other)
    conditioned = lax.all_gather(conditioned, "yh")
    conditioned = lax.all_gather(conditioned, ("z", "c")).reshape(16, 2, 2, 264, 128)

    partial = pl.pallas_call(
        score_kernel,
        out_shape=jax.ShapeDtypeStruct((8, 64, examples), BF16),
        in_specs=[vm, vm],
        out_specs=vm,
        scratch_shapes=[VMEM((512, grad), BF16)],
        compiler_params=grant(24),
    )(conditioned, stored)
    partial = lax.all_to_all(partial, ("x", "yl"), 0, 0, tiled=True)
    return jnp.sum(partial.astype(F32), axis=0).T


def solution(mesh):
    fine = Mesh(mesh.devices.reshape(4, 2, 2, 16, 2), AXES)
    module, store = ("x", "yl"), ("yh", "z", "c")
    return jax.shard_map(
        body,
        mesh=fine,
        in_specs=(
            P(module, store, None),
            P(store, None),
            P(module, store, None),
            P(module, store, None),
        ),
        out_specs=P(store, module),
        check_vma=False,
    )
```
